32 devices in a mesh: chan: 16 (over z, x, core), tm: 2 (over y).
Axes of the slice: x: 2, y: 2, z: 4, core: 2. Of those that a mesh axis runs over, the one named last changes fastest.
Arguments:
- volt: bfloat16 [2, 64, 2048, 512], P(None, None, ('chan', 'tm')), may hold values from -40 to 40
- windows: int32 [64, 2], P('chan'), may hold values from 0 to 2048, as said below
- start_basis: float32 [2, 64, 8, 512], P(None, 'chan'), may hold values from -6 to 6
- positions: float32 [2, 512], replicated, may hold values from -16 to 16
- pointing: float32 [2, 1024], replicated, may hold values from -0.7 to 0.7
- beam_dir: int32 [1024], replicated, may hold values from 0 to 1023, each once
Outputs:
- power: float32 [64, 1024], P('chan', 'tm')
The draws below stay inside these ranges and needn't reach their ends.
Inputs may be any that keep to these rules, and one draw needn't show every extreme that they name: `windows`: each row holds a channel's first window sample and one past its last; every window holds 1024 samples or more. `beam_dir`: each table entry is named by exactly one beam.
All inputs are finite; a program needn't handle non-finite values.
Results may differ from the reference program's by a relative error of at most 0.0024.
Values may be sent and summed in bfloat16 or wider, within the bound.
No kernel may reach another device: no remote copies, remote signals or barrier semaphores. Data moves between devices by JAX's collectives and lax.ppermute only.
A program may use at most 128 MiB of HBM per device.

```python
import math
import jax
import jax.numpy as jnp
from jax import lax

S = 512
B = 1024
K = 8
ITERS = 6
NDIR = 1024
CH = 64
TIME = 2048


def geometry(key):
    shared = jax.random.fold_in(key, 7103)
    subkeys = jax.random.split(shared, 2)
    positions = jax.random.uniform(subkeys[0], (2, S), jnp.float32, -16.0, 16.0)
    pointing = jax.random.uniform(subkeys[1], (2, NDIR), jnp.float32, -0.7, 0.7)
    return (positions, pointing)


def draw_positions(key, part):
    return geometry(key)[0]


def draw_pointing(key, part):
    return geometry(key)[1]


def pick_directions(subkey):
    return jax.random.permutation(subkey, NDIR)[:K]


def draw_volt(key, part):
    positions, pointing = geometry(key)
    own = jax.random.fold_in(key, 2917)
    subkeys = jax.random.split(own, 5)
    background = jax.random.normal(subkeys[0], (2, CH, TIME, S), jnp.float32)
    weak_excess = jax.random.uniform(subkeys[1], (CH, K // 2), jnp.float32, 1.6, 3.5)
    strong_excess = jnp.exp(jax.random.uniform(subkeys[2], (CH, K - K // 2), jnp.float32, math.log(4.0), math.log(24.0)))
    excess = jnp.concatenate([weak_excess, strong_excess], axis=1)
    strength = excess / S
    chosen = jax.vmap(pick_directions)(jax.random.split(subkeys[3], CH))
    east_cos = pointing[0][chosen]
    north_cos = pointing[1][chosen]
    frequency = 1.0 + jnp.arange(CH, dtype=jnp.float32) / CH
    phases = (2.0 * math.pi * frequency)[:, None, None] * (positions[0][None, None, :] * east_cos[:, :, None] + positions[1][None, None, :] * north_cos[:, :, None])
    pattern_real = jnp.cos(phases)
    pattern_imag = jnp.sin(phases)
    signal = jax.random.normal(subkeys[4], (2, CH, TIME, K), jnp.float32)
    envelope = jnp.sqrt(strength)[:, None, :]
    sig_real = signal[0] * envelope
    sig_imag = signal[1] * envelope
    real_part = background[0] + jnp.einsum('ctr,crs->cts', sig_real, pattern_real) - jnp.einsum('ctr,crs->cts', sig_imag, pattern_imag)
    imag_part = background[1] + jnp.einsum('ctr,crs->cts', sig_real, pattern_imag) + jnp.einsum('ctr,crs->cts', sig_imag, pattern_real)
    stacked = jnp.stack([real_part, imag_part])
    return jnp.clip(stacked, -40.0, 40.0).astype(jnp.bfloat16)


def draw_windows(key, part):
    subkeys = jax.random.split(key, 2)
    length = jax.random.randint(subkeys[0], (CH, 1), TIME // 2, TIME + 1)
    offset = jax.random.randint(subkeys[1], (CH, 1), 0, TIME + 1) % (TIME - length + 1)
    return jnp.concatenate([offset, offset + length], axis=1).astype(jnp.int32)


def block_levels(own_key, extent, cuts, low, largest):
    def one(axis_at, shards_of):
        steps = jax.random.uniform(jax.random.fold_in(jax.random.fold_in(own_key, 6), axis_at), (shards_of,), jnp.float32, low / len(cuts), largest / len(cuts))
        return jnp.repeat(jnp.exp(steps), extent[axis_at] // shards_of).reshape((-1,) + (1,) * (len(extent) - axis_at - 1))

    gain = one(*cuts[0])
    for cut in cuts[1:]:
        gain = gain * one(*cut)
    return gain


def normal_values(stream_key, extent, width, most, cuts=(), held_as=jnp.bfloat16):
    entries = width * jax.random.normal(stream_key, extent, jnp.float32)
    if cuts:
        entries = entries * block_levels(stream_key, extent, cuts, -0.22, 0.18)
    return jnp.clip(entries, -most, most).astype(held_as)


def setup_inputs(seed: int = 0) -> dict:
    arg_keys = jax.random.split(jax.random.key(seed), 7)
    volt = draw_volt(jax.random.fold_in(arg_keys[6], 71), 0)
    windows = draw_windows(jax.random.fold_in(arg_keys[6], 71), 0)
    start_basis = normal_values(arg_keys[2], (2, CH, K, S), 1.0, 6.0, ((1, 16),), jnp.float32)
    positions = draw_positions(jax.random.fold_in(arg_keys[6], 71), 0)
    pointing = draw_pointing(jax.random.fold_in(arg_keys[6], 71), 0)
    beam_dir = jax.random.permutation(arg_keys[5], B).astype(jnp.int32)
    return {"volt": volt, "windows": windows, "start_basis": start_basis, "positions": positions, "pointing": pointing, "beam_dir": beam_dir}


EPS = 1e-06
TWO_PI = 2.0 * math.pi

def orthonormal(real_part, imag_part):
    number = real_part.shape[-2]
    base_real = []
    base_imag = []
    for column in range(number):
        vec_real = real_part[..., column, :]
        vec_imag = imag_part[..., column, :]
        for earlier in range(column):
            prev_real = base_real[earlier]
            prev_imag = base_imag[earlier]
            coef_real = lax.optimization_barrier(jnp.sum(prev_real * vec_real + prev_imag * vec_imag, axis=-1, keepdims=True))
            coef_imag = lax.optimization_barrier(jnp.sum(prev_real * vec_imag - prev_imag * vec_real, axis=-1, keepdims=True))
            vec_real = vec_real - (coef_real * prev_real - coef_imag * prev_imag)
            vec_imag = vec_imag - (coef_real * prev_imag + coef_imag * prev_real)
        inverse = lax.rsqrt(lax.optimization_barrier(jnp.sum(vec_real * vec_real + vec_imag * vec_imag, axis=-1, keepdims=True)) + EPS)
        base_real.append(vec_real * inverse)
        base_imag.append(vec_imag * inverse)
    return (jnp.stack(base_real, axis=-2), jnp.stack(base_imag, axis=-2))

def fdot(left, right):
    return jnp.dot(left, right, preferred_element_type=jnp.float32)

def subspace(volt_real, volt_imag, window_mask, basis_real, basis_imag):
    base_real, base_imag = orthonormal(basis_real, basis_imag)
    for iteration in range(ITERS):
        low_real = base_real.astype(jnp.bfloat16)
        low_imag = base_imag.astype(jnp.bfloat16)
        proj_real = fdot(volt_real, low_real.T) + fdot(volt_imag, low_imag.T)
        proj_imag = fdot(volt_imag, low_real.T) - fdot(volt_real, low_imag.T)
        proj_real = (proj_real * window_mask[:, None]).astype(jnp.bfloat16)
        proj_imag = (proj_imag * window_mask[:, None]).astype(jnp.bfloat16)
        image_real = fdot(proj_real.T, volt_real) - fdot(proj_imag.T, volt_imag)
        image_imag = fdot(proj_real.T, volt_imag) + fdot(proj_imag.T, volt_real)
        base_real, base_imag = orthonormal(image_real, image_imag)
    return (base_real, base_imag)

def channel_power(volt_real, volt_imag, base_real, base_imag, freq, direction, positions):
    low_real = base_real.astype(jnp.bfloat16)
    low_imag = base_imag.astype(jnp.bfloat16)
    full_real = (fdot(volt_real, low_real.T) + fdot(volt_imag, low_imag.T)).astype(jnp.bfloat16)
    full_imag = (fdot(volt_imag, low_real.T) - fdot(volt_real, low_imag.T)).astype(jnp.bfloat16)
    removed_real = fdot(full_real, low_real) - fdot(full_imag, low_imag)
    removed_imag = fdot(full_real, low_imag) + fdot(full_imag, low_real)
    clean_real = (volt_real.astype(jnp.float32) - removed_real).astype(jnp.bfloat16)
    clean_imag = (volt_imag.astype(jnp.float32) - removed_imag).astype(jnp.bfloat16)
    phase = TWO_PI * freq * (positions[0][:, None] * direction[0][None, :] + positions[1][:, None] * direction[1][None, :])
    steer_real = jnp.cos(phase).astype(jnp.bfloat16)
    steer_imag = jnp.sin(phase).astype(jnp.bfloat16)
    beam_real = fdot(clean_real, steer_real) + fdot(clean_imag, steer_imag)
    beam_imag = fdot(clean_imag, steer_real) - fdot(clean_real, steer_imag)
    return lax.optimization_barrier(jnp.sum(beam_real * beam_real + beam_imag * beam_imag, axis=0))

def reference(volt, windows, start_basis, positions, pointing, beam_dir):
    samples = jnp.arange(TIME, dtype=jnp.int32)
    direction = jnp.take(pointing, beam_dir, axis=1)

    def one_channel(channel):
        volt_real = volt[0, channel]
        volt_imag = volt[1, channel]
        window_mask = ((samples >= windows[channel, 0]) & (samples < windows[channel, 1])).astype(jnp.float32)
        base_real, base_imag = subspace(volt_real, volt_imag, window_mask, start_basis[0, channel], start_basis[1, channel])
        freq = 1.0 + channel.astype(jnp.float32) / CH
        return channel_power(volt_real, volt_imag, base_real, base_imag, freq, direction, positions)
    power = lax.map(one_channel, jnp.arange(CH, dtype=jnp.int32))
    return power / (TIME * S)
```

```python
import functools

import jax
import jax.numpy as jnp
import numpy as np
from jax import lax
from jax.experimental import pallas as pl
from jax.experimental.pallas import tpu as pltpu
from jax.sharding import Mesh
from jax.sharding import PartitionSpec as P

ITERS = 6
EPS = 1e-06
F32 = jnp.float32
BF16 = jnp.bfloat16
VMEM = pl.BlockSpec(memory_space=pltpu.VMEM)
SMEM = pl.BlockSpec(memory_space=pltpu.SMEM)
VMEM_LIMIT = 40 << 20


def orthonormal(chans):
    number = chans[0][0].shape[0]
    row = lax.broadcasted_iota(jnp.int32, (number, 1), 0)
    for j in range(number):
        after = []
        for re, im in chans:
            top_re, top_im = re[j : j + 1], im[j : j + 1]
            dot_re = jnp.sum(top_re * re + top_im * im, axis=1, keepdims=True)
            dot_im = jnp.sum(top_re * im - top_im * re, axis=1, keepdims=True)
            inverse = lax.rsqrt(dot_re[j : j + 1] + EPS)
            share = jnp.where(row > j, inverse * inverse, 0.0)
            coef_re, coef_im = share * dot_re, share * dot_im
            scale = jnp.where(row == j, inverse, 1.0)
            after.append(
                (
                    re * scale - (coef_re * top_re - coef_im * top_im),
                    im * scale - (coef_re * top_im + coef_im * top_re),
                )
            )
        chans = after
    return chans


def contract(left, right, at_left, at_right):
    return lax.dot_general(
        left, right, (((at_left,), (at_right,)), ((), ())), preferred_element_type=F32
    )


def project(base_re, base_im, volt_re, volt_im):
    first = jnp.concatenate([base_re, -base_im], 0).astype(BF16)
    second = jnp.concatenate([base_im, base_re], 0).astype(BF16)
    return contract(first, volt_re, 1, 1) + contract(second, volt_im, 1, 1)


def split(stacked):
    number = stacked.shape[0] // 2
    return stacked[:number], stacked[number:]


def iterate_kernel(first, win_ref, start_ref, *refs):
    *image_refs, volt_ref, out_ref = refs
    sources, _, channels, rows, stations = volt_ref.shape
    number = out_ref.shape[1] // 2
    total = sources * rows
    chans = []
    for c in range(channels):
        stacked = image_refs[0][c] if first else image_refs[0][c] + image_refs[1][c]
        chans.append(split(stacked))
    chans = orthonormal(chans)
    sample = start_ref[0] + lax.broadcasted_iota(jnp.int32, (1, total), 1)
    for c in range(channels):
        volt_re = volt_ref[:, 0, c].reshape(total, stations)
        volt_im = volt_ref[:, 1, c].reshape(total, stations)
        proj = project(*chans[c], volt_re, volt_im)
        inside = (sample >= win_ref[c, 0]) & (sample < win_ref[c, 1])
        proj = jnp.where(inside, proj, 0.0).astype(BF16)
        by_re = contract(proj, volt_re, 1, 0)
        by_im = contract(proj, volt_im, 1, 0)
        out_ref[c, :number] = by_re[:number] - by_im[number:]
        out_ref[c, number:] = by_im[:number] + by_re[number:]


def iterate(windows, start, images, volt):
    first = len(images) == 1
    channels = images[0].shape[0]
    return pl.pallas_call(
        functools.partial(iterate_kernel, first),
        out_shape=jax.ShapeDtypeStruct(images[0].shape, F32),
        in_specs=[SMEM, SMEM] + [VMEM] * (len(images) + 1),
        out_specs=VMEM,
        compiler_params=pltpu.CompilerParams(vmem_limit_bytes=VMEM_LIMIT),
        cost_estimate=pl.CostEstimate(
            flops=volt.size * 64, bytes_accessed=volt.size * 2, transcendentals=0
        ),
        name="iterate",
    )(windows, start, *images, volt)


def beam_kernel(at, own_ref, other_ref, volt_ref, steer_ref, out_ref, clean_ref):
    sources, _, _, rows, stations = volt_ref.shape
    total = sources * rows

    @pl.when(pl.program_id(0) == 0)
    def _():
        ((base_re, base_im),) = orthonormal([split(own_ref[at] + other_ref[at])])
        volt_re = volt_ref[:, 0, 0].reshape(total, stations)
        volt_im = volt_ref[:, 1, 0].reshape(total, stations)
        full = project(base_re, base_im, volt_re, volt_im).astype(BF16)
        low_re = jnp.concatenate([base_re, -base_im], 0).astype(BF16)
        low_im = jnp.concatenate([base_im, base_re], 0).astype(BF16)
        clean_ref[0] = (volt_re.astype(F32) - contract(full, low_re, 0, 0)).astype(BF16)
        clean_ref[1] = (volt_im.astype(F32) - contract(full, low_im, 0, 0)).astype(BF16)

    clean_re, clean_im = clean_ref[0], clean_ref[1]
    steer_re, steer_im = steer_ref[0, 0], steer_ref[0, 1]
    beam_re = contract(clean_re, steer_re, 1, 0) + contract(clean_im, steer_im, 1, 0)
    beam_im = contract(clean_im, steer_re, 1, 0) - contract(clean_re, steer_im, 1, 0)
    out_ref[0] = jnp.sum(beam_re * beam_re + beam_im * beam_im, axis=0, keepdims=True)


def beam_power(at, images, volt, steer, channel, tile):
    own, other = images
    sources, parts, _, rows, stations = volt.shape
    beams = steer.shape[-1]
    whole = pl.BlockSpec(own.shape, lambda i: (0, 0, 0))
    return pl.pallas_call(
        functools.partial(beam_kernel, at),
        out_shape=jax.ShapeDtypeStruct((1, 1, beams), F32),
        grid=(beams // tile,),
        in_specs=[
            whole,
            whole,
            pl.BlockSpec((sources, parts, 1, rows, stations), lambda i: (0, 0, at, 0, 0)),
            pl.BlockSpec((1, parts, stations, tile), lambda i: (channel, 0, 0, i)),
        ],
        out_specs=pl.BlockSpec((1, 1, tile), lambda i: (0, 0, i)),
        scratch_shapes=[pltpu.VMEM((parts, sources * rows, stations), BF16)],
        compiler_params=pltpu.CompilerParams(vmem_limit_bytes=VMEM_LIMIT),
        cost_estimate=pl.CostEstimate(
            flops=sources * rows * stations * beams * 8,
            bytes_accessed=stations * beams * 4,
            transcendentals=0,
        ),
        name="beams",
    )(own, other, volt, steer)


def turn_series():
    nodes = np.cos((np.arange(4000) + 0.5) / 4000 * np.pi) * 0.25 + 0.25
    angle = 2.0 * np.pi * nodes
    fit = np.polynomial.chebyshev.Chebyshev.fit
    made = []
    for values, degree in ((np.cos(angle), 7), (np.sin(angle) / nodes, 6)):
        series = fit(nodes * nodes, values, degree, domain=[0, 0.25])
        made.append(series.convert(kind=np.polynomial.Polynomial).coef)
    return made


COS_SERIES, SIN_SERIES = turn_series()


def horner(at, series):
    total = jnp.float32(series[-1]) * at + jnp.float32(series[-2])
    for coef in series[-3::-1]:
        total = total * at + jnp.float32(coef)
    return total


def steer_kernel(freq_ref, place_ref, toward_ref, out_ref):
    delay = place_ref[:, 0:1] * toward_ref[0:1, :] + place_ref[:, 1:2] * toward_ref[1:2, :]
    for c in range(out_ref.shape[0]):
        turns = delay * freq_ref[c]
        rest = turns - jnp.round(turns)
        square = rest * rest
        out_ref[c, 0] = horner(square, COS_SERIES).astype(BF16)
        out_ref[c, 1] = (rest * horner(square, SIN_SERIES)).astype(BF16)


def steering(freq, places, toward, tile):
    channels, stations, beams = freq.shape[0], places.shape[0], toward.shape[1]
    return pl.pallas_call(
        steer_kernel,
        out_shape=jax.ShapeDtypeStruct((channels, 2, stations, beams), BF16),
        grid=(beams // tile,),
        in_specs=[
            SMEM,
            pl.BlockSpec((stations, 2), lambda i: (0, 0)),
            pl.BlockSpec((2, tile), lambda i: (0, i)),
        ],
        out_specs=pl.BlockSpec((channels, 2, stations, tile), lambda i: (0, 0, 0, i)),
        compiler_params=pltpu.CompilerParams(vmem_limit_bytes=VMEM_LIMIT),
        cost_estimate=pl.CostEstimate(
            flops=channels * stations * beams * 40,
            bytes_accessed=channels * stations * beams * 4,
            transcendentals=0,
        ),
        name="steering",
    )(freq, places, toward)


SWAP = [(0, 1), (1, 0)]


def body(volt, windows, start_basis, positions, pointing, beam_dir):
    parts, channels_all, rows, stations = volt.shape
    number = start_basis.shape[2]
    n_lo, n_time = lax.axis_size("lo"), lax.axis_size("tm")
    half_at, lo_at, time_at = (lax.axis_index(a) for a in ("hi", "lo", "tm"))
    group = n_lo * n_time
    chan_dev = windows.shape[0]
    per = chan_dev // n_time
    half_time = rows * group
    beams = beam_dir.shape[0]

    blocks = volt.reshape(parts, 2, group, per, rows, stations)
    chunks = [(0, tuple(range(per)))] + [(1, (i,)) for i in range(per)]
    moved = []
    for owner, members in chunks:
        picked = blocks[:, owner, :, members[0] : members[-1] + 1]
        picked = jnp.transpose(picked, (1, 0, 2, 3, 4))
        moved.append(lax.all_to_all(picked, ("lo", "tm"), split_axis=0, concat_axis=0, tiled=True))

    own_windows = lax.dynamic_slice_in_dim(windows, time_at * per, per, 0)
    own_basis = lax.dynamic_slice_in_dim(start_basis, time_at * per, per, 1)
    own_basis = jnp.transpose(own_basis, (1, 0, 2, 3)).reshape(per, parts * number, stations)
    far_windows = lax.ppermute(own_windows, "hi", SWAP)
    far_basis = lax.ppermute(own_basis, "hi", SWAP)
    lower = half_at == 0
    all_windows = [
        jnp.where(lower, own_windows, far_windows),
        jnp.where(lower, far_windows, own_windows),
    ]
    all_basis = [jnp.where(lower, own_basis, far_basis), jnp.where(lower, far_basis, own_basis)]
    first_sample = (half_at * half_time).astype(jnp.int32).reshape(1)

    toward = jnp.take(pointing, beam_dir, axis=1)
    channel_ids = jnp.stack(
        [
            (owner * n_lo + lo_at) * chan_dev + time_at * per + i
            for owner in range(2)
            for i in range(per)
        ]
    )
    freq = 1.0 + channel_ids.astype(F32) / channels_all
    steer = steering(freq, positions.T, toward, 128)

    power = []
    for (owner, members), local in zip(chunks, moved, strict=True):
        pick = slice(members[0], members[-1] + 1)
        win = all_windows[owner][pick]
        images = (all_basis[owner][pick],)
        for _ in range(ITERS):
            image = iterate(win, first_sample, images, local)
            images = (image, lax.ppermute(image, "hi", SWAP))
        for at, member in enumerate(members):
            power.append(beam_power(at, images, local, steer, owner * per + member, min(512, beams)))
    mine = jnp.stack(power).reshape(2, per, n_time, beams // n_time)
    mine = jnp.transpose(mine, (0, 2, 1, 3)) / (2 * half_time * stations)
    flat = mine.reshape(2 * n_time, per, beams // n_time)
    came = lax.all_to_all(flat, ("hi", "tm"), split_axis=0, concat_axis=0, tiled=True)
    came = came.reshape(2, n_time * per, beams // n_time)
    return came[0] + came[1]


def solution(mesh):
    n_chan, n_time = mesh.shape["chan"], mesh.shape["tm"]
    halves = Mesh(mesh.devices.reshape(2, n_chan // 2, n_time), ("hi", "lo", "tm"))
    chan = ("hi", "lo")
    return jax.shard_map(
        body,
        mesh=halves,
        in_specs=(
            P(None, None, ("hi", "lo", "tm"), None),
            P(chan, None),
            P(None, chan, None, None),
            P(),
            P(),
            P(),
        ),
        out_specs=P(chan, "tm"),
        check_vma=False,
    )
```

```python
import functools

import jax
import jax.numpy as jnp
import numpy as np
from jax import lax
from jax.experimental import pallas as pl
from jax.experimental.pallas import tpu as pltpu
from jax.sharding import Mesh
from jax.sharding import PartitionSpec as P

ITERS = 6
EPS = 1e-06
F32 = jnp.float32
BF16 = jnp.bfloat16
VMEM = pl.BlockSpec(memory_space=pltpu.VMEM)
SMEM = pl.BlockSpec(memory_space=pltpu.SMEM)
ANY = pl.BlockSpec(memory_space=pl.ANY)
VMEM_LIMIT = 40 << 20


def orthonormal(chans):
    number = chans[0][0].shape[0]
    row = lax.broadcasted_iota(jnp.int32, (number, 1), 0)
    for j in range(number):
        after = []
        for re, im in chans:
            top_re, top_im = re[j : j + 1], im[j : j + 1]
            dot_re = jnp.sum(top_re * re + top_im * im, axis=1, keepdims=True)
            dot_im = jnp.sum(top_re * im - top_im * re, axis=1, keepdims=True)
            inverse = lax.rsqrt(dot_re[j : j + 1] + EPS)
            share = jnp.where(row > j, inverse * inverse, 0.0)
            coef_re, coef_im = share * dot_re, share * dot_im
            scale = jnp.where(row == j, inverse, 1.0)
            after.append(
                (
                    re * scale - (coef_re * top_re - coef_im * top_im),
                    im * scale - (coef_re * top_im + coef_im * top_re),
                )
            )
        chans = after
    return chans


def contract(left, right, at_left, at_right):
    return lax.dot_general(
        left, right, (((at_left,), (at_right,)), ((), ())), preferred_element_type=F32
    )


def project(base_re, base_im, volt_re, volt_im):
    first = jnp.concatenate([base_re, -base_im], 0).astype(BF16)
    second = jnp.concatenate([base_im, base_re], 0).astype(BF16)
    return contract(first, volt_re, 1, 1) + contract(second, volt_im, 1, 1)


def split(stacked):
    number = stacked.shape[0] // 2
    return stacked[:number], stacked[number:]


def images_of(image_refs, at):
    total = image_refs[0][at].astype(F32)
    for ref in image_refs[1:]:
        total = total + ref[at].astype(F32)
    return split(total)


def channels_of(volt_refs):
    for ref in volt_refs:
        sources, _, members, rows, stations = ref.shape
        for m in range(members):
            yield tuple(ref[:, part, m].reshape(sources * rows, stations) for part in range(2))


def iterate_kernel(n_images, n_volt, win_ref, start_ref, *refs):
    image_refs, volt_refs, out_ref = refs[:n_images], refs[n_images : n_images + n_volt], refs[-1]
    channels, number = out_ref.shape[0], out_ref.shape[1] // 2
    total = volt_refs[0].shape[0] * volt_refs[0].shape[3]
    bases = orthonormal([images_of(image_refs, c) for c in range(channels)])
    sample = start_ref[0] + lax.broadcasted_iota(jnp.int32, (1, total), 1)
    for c, (volt_re, volt_im) in enumerate(channels_of(volt_refs)):
        proj = project(*bases[c], volt_re, volt_im)
        inside = (sample >= win_ref[c, 0]) & (sample < win_ref[c, 1])
        proj = jnp.where(inside, proj, 0.0).astype(BF16)
        by_re = contract(proj, volt_re, 1, 0)
        by_im = contract(proj, volt_im, 1, 0)
        out_ref[c, :number] = (by_re[:number] - by_im[number:]).astype(out_ref.dtype)
        out_ref[c, number:] = (by_im[:number] + by_re[number:]).astype(out_ref.dtype)


def iterate(windows, start, images, volts, after):
    moved = sum(v.size for v in volts)
    return pl.pallas_call(
        functools.partial(iterate_kernel, len(images), len(volts)),
        out_shape=jax.ShapeDtypeStruct(images[0].shape, BF16),
        in_specs=[SMEM, SMEM] + [VMEM] * (len(images) + len(volts)) + [ANY] * len(after),
        out_specs=VMEM,
        compiler_params=pltpu.CompilerParams(vmem_limit_bytes=VMEM_LIMIT),
        cost_estimate=pl.CostEstimate(
            flops=moved * 64, bytes_accessed=moved * 2, transcendentals=0
        ),
        name="iterate",
    )(windows, start, *images, *volts, *after)


def raw_kernel(volt_ref, steer_ref, *refs):
    out_ref = refs[-1]
    ((volt_re, volt_im),) = channels_of([volt_ref])
    steer_re, steer_im = steer_ref[0, 0], steer_ref[0, 1]
    beam_re = contract(volt_re, steer_re, 1, 0) + contract(volt_im, steer_im, 1, 0)
    beam_im = contract(volt_im, steer_re, 1, 0) - contract(volt_re, steer_im, 1, 0)
    out_ref[0] = jnp.sum(beam_re * beam_re + beam_im * beam_im, axis=0, keepdims=True)


def raw_power(volt, at, steer, channel, first, width, tile, after):
    sources, parts, _, rows, stations = volt.shape
    return pl.pallas_call(
        raw_kernel,
        out_shape=jax.ShapeDtypeStruct((1, 1, width), F32),
        grid=(width // tile,),
        in_specs=[
            pl.BlockSpec((sources, parts, 1, rows, stations), lambda i: (0, 0, at, 0, 0)),
            pl.BlockSpec(
                (1, parts, stations, tile), lambda i: (channel, 0, 0, first // tile + i)
            ),
        ]
        + [ANY] * len(after),
        out_specs=pl.BlockSpec((1, 1, tile), lambda i: (0, 0, i)),
        compiler_params=pltpu.CompilerParams(vmem_limit_bytes=VMEM_LIMIT),
        cost_estimate=pl.CostEstimate(
            flops=sources * rows * stations * width * 8,
            bytes_accessed=stations * width * 4,
            transcendentals=0,
        ),
        name="raw_power",
    )(volt, steer, *after)


def null_kernel(n_volt, own_ref, other_ref, raw_ref, steer_ref, *refs):
    volt_refs, out_ref, base_ref = refs[:n_volt], refs[n_volt], refs[n_volt + 1]
    channels = own_ref.shape[0]

    @pl.when(pl.program_id(0) == 0)
    def _():
        made = orthonormal([images_of((own_ref, other_ref), c) for c in range(channels)])
        for c, (base_re, base_im) in enumerate(made):
            base_ref[c] = jnp.concatenate([base_re, base_im], 0)

    for c, (volt_re, volt_im) in enumerate(channels_of(volt_refs)):

        @pl.when(pl.program_id(0) == c)
        def _(c=c, volt_re=volt_re, volt_im=volt_im):
            base = base_ref[c]
            base_re, base_im = split(base)
            number = base_re.shape[0]
            full = project(base_re, base_im, volt_re, volt_im).astype(BF16)
            by_re, by_im = contract(full, volt_re, 1, 0), contract(full, volt_im, 1, 0)
            met = jnp.concatenate(
                [by_re[:number] + by_im[number:], by_re[number:] - by_im[:number]], 0
            )
            high = met.astype(BF16)
            low = (met - high.astype(F32)).astype(BF16)
            left = jnp.concatenate([base.astype(BF16), high, low], 0)
            on_re = contract(left, steer_ref[0, 0], 1, 0)
            on_im = contract(left, steer_ref[0, 1], 1, 0)
            base_on_re, base_on_im = on_re[: 2 * number], on_im[: 2 * number]
            met_on_re = on_re[2 * number : 4 * number] + on_re[4 * number :]
            met_on_im = on_im[2 * number : 4 * number] + on_im[4 * number :]
            gain_re = base_on_re[:number] + base_on_im[number:]
            gain_im = base_on_re[number:] - base_on_im[:number]
            met_re = met_on_re[:number] - met_on_im[number:]
            met_im = met_on_im[:number] + met_on_re[number:]
            pairs = contract(full, full, 1, 1)
            pair_re = pairs[:number, :number] + pairs[number:, number:]
            pair_im = pairs[:number, number:] - pairs[number:, :number]
            taken_re, taken_im = -2.0 * met_re, 2.0 * met_im
            for k in range(number):
                top_re, top_im = gain_re[k : k + 1], gain_im[k : k + 1]
                at_re, at_im = pair_re[:, k : k + 1], pair_im[:, k : k + 1]
                taken_re = taken_re + (at_re * top_re - at_im * top_im)
                taken_im = taken_im + (at_re * top_im + at_im * top_re)
            change = jnp.sum(gain_re * taken_re + gain_im * taken_im, axis=0, keepdims=True)
            out_ref[0] = raw_ref[0] + change


def nulled_power(images, raw, volts, steer):
    own, other = images
    channels, parts, stations, beams = steer.shape
    moved = sum(v.size for v in volts)
    same = lambda v: pl.BlockSpec(v.shape, lambda i: (0,) * len(v.shape))
    return pl.pallas_call(
        functools.partial(null_kernel, len(volts)),
        out_shape=jax.ShapeDtypeStruct((channels, 1, beams), F32),
        grid=(channels,),
        in_specs=[
            same(own),
            same(other),
            pl.BlockSpec((1, 1, beams), lambda i: (i, 0, 0)),
            pl.BlockSpec((1, parts, stations, beams), lambda i: (i, 0, 0, 0)),
        ]
        + [VMEM] * len(volts),
        out_specs=pl.BlockSpec((1, 1, beams), lambda i: (i, 0, 0)),
        scratch_shapes=[pltpu.VMEM(own.shape, F32)],
        compiler_params=pltpu.CompilerParams(vmem_limit_bytes=VMEM_LIMIT),
        cost_estimate=pl.CostEstimate(
            flops=moved * 64 + steer.size * 96,
            bytes_accessed=moved * 2 + steer.size * 2,
            transcendentals=0,
        ),
        name="nulled_power",
    )(own, other, raw, steer, *volts)


def turn_series():
    nodes = np.cos((np.arange(4000) + 0.5) / 4000 * np.pi) * 0.25 + 0.25
    angle = 2.0 * np.pi * nodes
    fit = np.polynomial.chebyshev.Chebyshev.fit
    made = []
    for values, degree in ((np.cos(angle), 7), (np.sin(angle) / nodes, 6)):
        series = fit(nodes * nodes, values, degree, domain=[0, 0.25])
        made.append(series.convert(kind=np.polynomial.Polynomial).coef)
    return made


COS_SERIES, SIN_SERIES = turn_series()


def horner(at, series):
    total = jnp.float32(series[-1]) * at + jnp.float32(series[-2])
    for coef in series[-3::-1]:
        total = total * at + jnp.float32(coef)
    return total


def steer_kernel(freq_ref, place_ref, toward_ref, out_ref):
    delay = place_ref[:, 0:1] * toward_ref[0:1, :] + place_ref[:, 1:2] * toward_ref[1:2, :]
    for c in range(out_ref.shape[0]):
        turns = delay * freq_ref[c]
        rest = turns - jnp.round(turns)
        square = rest * rest
        out_ref[c, 0] = horner(square, COS_SERIES).astype(BF16)
        out_ref[c, 1] = (rest * horner(square, SIN_SERIES)).astype(BF16)


def steering(freq, places, toward, tile):
    channels, stations, beams = freq.shape[0], places.shape[0], toward.shape[1]
    return pl.pallas_call(
        steer_kernel,
        out_shape=jax.ShapeDtypeStruct((channels, 2, stations, beams), BF16),
        grid=(beams // tile,),
        in_specs=[
            SMEM,
            pl.BlockSpec((stations, 2), lambda i: (0, 0)),
            pl.BlockSpec((2, tile), lambda i: (0, i)),
        ],
        out_specs=pl.BlockSpec((channels, 2, stations, tile), lambda i: (0, 0, 0, i)),
        compiler_params=pltpu.CompilerParams(vmem_limit_bytes=VMEM_LIMIT),
        cost_estimate=pl.CostEstimate(
            flops=channels * stations * beams * 40,
            bytes_accessed=channels * stations * beams * 4,
            transcendentals=0,
        ),
        name="steering",
    )(freq, places, toward)


SWAP = [(0, 1), (1, 0)]


def body(volt, windows, start_basis, positions, pointing, beam_dir):
    parts, channels_all, rows, stations = volt.shape
    number = start_basis.shape[2]
    n_lo, n_time = lax.axis_size("lo"), lax.axis_size("tm")
    half_at, lo_at, time_at = (lax.axis_index(a) for a in ("hi", "lo", "tm"))
    group = n_lo * n_time
    chan_dev = windows.shape[0]
    per = chan_dev // n_time
    half_time = rows * group
    beams = beam_dir.shape[0]

    blocks = volt.reshape(parts, 2, group, per, rows, stations)
    volts = []
    for owner in range(2):
        picked = jnp.transpose(blocks[:, owner], (1, 0, 2, 3, 4))
        volts.append(lax.all_to_all(picked, ("lo", "tm"), split_axis=0, concat_axis=0, tiled=True))

    own_windows = lax.dynamic_slice_in_dim(windows, time_at * per, per, 0)
    own_basis = lax.dynamic_slice_in_dim(start_basis, time_at * per, per, 1)
    own_basis = jnp.transpose(own_basis, (1, 0, 2, 3)).reshape(per, parts * number, stations)
    far_windows = lax.ppermute(own_windows, "hi", SWAP)
    far_basis = lax.ppermute(own_basis, "hi", SWAP)
    lower = half_at == 0

    def by_owner(own, far):
        return jnp.concatenate([jnp.where(lower, own, far), jnp.where(lower, far, own)])

    all_windows = by_owner(own_windows, far_windows)
    images = (by_owner(own_basis, far_basis),)
    first_sample = (half_at * half_time).astype(jnp.int32).reshape(1)

    toward = jnp.take(pointing, beam_dir, axis=1)
    ids = jnp.arange(per, dtype=jnp.int32) + (lo_at * chan_dev + time_at * per)
    channel_ids = jnp.concatenate([ids, ids + n_lo * chan_dev])
    freq = 1.0 + channel_ids.astype(F32) / channels_all
    steer = steering(freq, positions.T, toward, 128)

    wide = beams // 2
    tile = min(512, wide)
    raw = [
        raw_power(volts[0], i, steer, i, first, wide, tile, ())
        for i in range(per)
        for first in (0, wide)
    ]
    waiting = [(i, first) for i in range(per) for first in (0, wide)]
    after = ()
    for step in range(ITERS):
        image = iterate(all_windows, first_sample, images, volts, after)
        images = (image, lax.ppermute(image, "hi", SWAP))
        after = ()
        share = -(-len(waiting) // (ITERS - step))
        for i, first in waiting[:share]:
            made = raw_power(volts[1], i, steer, per + i, first, wide, tile, (image,))
            raw.append(made)
            after += (made,)
        waiting = waiting[share:]
    raw = jnp.concatenate(raw).reshape(2 * per, 1, beams)
    power = nulled_power(images, raw, volts, steer)
    mine = power.reshape(2, per, n_time, beams // n_time)
    mine = jnp.transpose(mine, (0, 2, 1, 3)) / (2 * half_time * stations)
    flat = mine.reshape(2 * n_time, per, beams // n_time)
    came = lax.all_to_all(flat, ("hi", "tm"), split_axis=0, concat_axis=0, tiled=True)
    came = came.reshape(2, n_time * per, beams // n_time)
    return came[0] + came[1]


def solution(mesh):
    n_chan, n_time = mesh.shape["chan"], mesh.shape["tm"]
    halves = Mesh(mesh.devices.reshape(2, n_chan // 2, n_time), ("hi", "lo", "tm"))
    chan = ("hi", "lo")
    return jax.shard_map(
        body,
        mesh=halves,
        in_specs=(
            P(None, None, ("hi", "lo", "tm"), None),
            P(chan, None),
            P(None, chan, None, None),
            P(),
            P(),
            P(),
        ),
        out_specs=P(chan, "tm"),
        check_vma=False,
    )
```

```python
import functools

import jax
import jax.numpy as jnp
import numpy as np
from jax import lax
from jax.experimental import pallas as pl
from jax.experimental.pallas import tpu as pltpu
from jax.sharding import Mesh
from jax.sharding import PartitionSpec as P

ITERS = 6
EPS = 1e-06
QUARTERS = 4
F32 = jnp.float32
BF16 = jnp.bfloat16
VMEM = pl.BlockSpec(memory_space=pltpu.VMEM)
SMEM = pl.BlockSpec(memory_space=pltpu.SMEM)
ANY = pl.BlockSpec(memory_space=pl.ANY)
VMEM_LIMIT = 24 << 20


def orthonormal(chans):
    number = chans[0][0].shape[0]
    row = lax.broadcasted_iota(jnp.int32, (number, 1), 0)
    for j in range(number):
        after = []
        for re, im in chans:
            top_re, top_im = re[j : j + 1], im[j : j + 1]
            dot_re = jnp.sum(top_re * re + top_im * im, axis=1, keepdims=True)
            dot_im = jnp.sum(top_re * im - top_im * re, axis=1, keepdims=True)
            inverse = lax.rsqrt(dot_re[j : j + 1] + EPS)
            share = jnp.where(row > j, inverse * inverse, 0.0)
            coef_re, coef_im = share * dot_re, share * dot_im
            scale = jnp.where(row == j, inverse, 1.0)
            after.append(
                (
                    re * scale - (coef_re * top_re - coef_im * top_im),
                    im * scale - (coef_re * top_im + coef_im * top_re),
                )
            )
        chans = after
    return chans


def contract(left, right, at_left, at_right):
    return lax.dot_general(
        left, right, (((at_left,), (at_right,)), ((), ())), preferred_element_type=F32
    )


def project(base_re, base_im, volt_re, volt_im):
    first = jnp.concatenate([base_re, -base_im], 0).astype(BF16)
    second = jnp.concatenate([base_im, base_re], 0).astype(BF16)
    return contract(first, volt_re, 1, 1) + contract(second, volt_im, 1, 1)


def split(stacked):
    number = stacked.shape[0] // 2
    return stacked[:number], stacked[number:]


def images_of(image_refs, at):
    total = image_refs[0][at].astype(F32)
    for ref in image_refs[1:]:
        total = total + ref[at].astype(F32)
    return split(total)


def params(limit=VMEM_LIMIT):
    return pltpu.CompilerParams(vmem_limit_bytes=limit)


def cost(flops, moved):
    return pl.CostEstimate(flops=int(flops), bytes_accessed=int(moved), transcendentals=0)


def pack_kernel(n_blocks, *refs):
    block_refs, out_ref = refs[:n_blocks], refs[-1]
    parts, owners, per, rows, _ = block_refs[0].shape
    for j, ref in enumerate(block_refs):
        for owner in range(owners):
            for i in range(per):
                for part in range(parts):
                    out_ref[owner * per + i, part, j * rows : (j + 1) * rows] = ref[part, owner, i]


def pack(blocks, after):
    parts, owners, per, rows, stations = blocks[0].shape
    shape = (owners * per, parts, len(blocks) * rows, stations)
    return pl.pallas_call(
        functools.partial(pack_kernel, len(blocks)),
        out_shape=jax.ShapeDtypeStruct(shape, BF16),
        in_specs=[VMEM] * len(blocks) + [ANY] * len(after),
        out_specs=VMEM,
        compiler_params=params(),
        cost_estimate=cost(0, 4 * len(blocks) * blocks[0].size),
        name="pack",
    )(*blocks, *after)


def iterate_kernel(n_images, n_volt, win_ref, *refs):
    image_refs, times_ref = refs[:n_images], refs[n_images]
    volt_refs, out_ref = refs[n_images + 1 : n_images + 1 + n_volt], refs[-1]
    channels, number = out_ref.shape[0], out_ref.shape[1] // 2
    width = volt_refs[0].shape[2]
    bases = orthonormal([images_of(image_refs, c) for c in range(channels)])
    for c in range(channels):
        by_re = by_im = None
        for q, ref in enumerate(volt_refs):
            volt_re, volt_im = ref[c, 0], ref[c, 1]
            proj = project(*bases[c], volt_re, volt_im)
            sample = times_ref[:, q * width : (q + 1) * width]
            inside = (sample >= win_ref[c, 0]) & (sample < win_ref[c, 1])
            proj = jnp.where(inside, proj, 0.0).astype(BF16)
            more_re, more_im = contract(proj, volt_re, 1, 0), contract(proj, volt_im, 1, 0)
            by_re = more_re if by_re is None else by_re + more_re
            by_im = more_im if by_im is None else by_im + more_im
        out_ref[c, :number] = (by_re[:number] - by_im[number:]).astype(out_ref.dtype)
        out_ref[c, number:] = (by_im[:number] + by_re[number:]).astype(out_ref.dtype)


def iterate(windows, times, images, volts, after):
    moved = sum(v.size for v in volts)
    return pl.pallas_call(
        functools.partial(iterate_kernel, len(images), len(volts)),
        out_shape=jax.ShapeDtypeStruct(images[0].shape, BF16),
        in_specs=[SMEM] + [VMEM] * (len(images) + 1 + len(volts)) + [ANY] * len(after),
        out_specs=VMEM,
        compiler_params=params(),
        cost_estimate=cost(moved * 64, moved * 2),
        name="iterate",
    )(windows, *images, times, *volts, *after)


def raw_kernel(volt_ref, steer_ref, *refs):
    out_ref = refs[-1]
    _, parts, rows, stations = volt_ref.shape
    volt = volt_ref[0].reshape(parts * rows, stations)
    on_re, on_im = contract(volt, steer_ref[0, 0], 1, 0), contract(volt, steer_ref[0, 1], 1, 0)
    beam_re = on_re[:rows] + on_im[rows:]
    beam_im = on_re[rows:] - on_im[:rows]
    out_ref[0] = jnp.sum(beam_re * beam_re + beam_im * beam_im, axis=0, keepdims=True)


def raw_power(volt, steer, after):
    channels, parts, rows, stations = volt.shape
    beams = steer.shape[-1]
    tile = min(512, beams)
    return pl.pallas_call(
        raw_kernel,
        out_shape=jax.ShapeDtypeStruct((channels, 1, beams), F32),
        grid=(channels, beams // tile),
        in_specs=[
            pl.BlockSpec((1, parts, rows, stations), lambda c, i: (c, 0, 0, 0)),
            pl.BlockSpec((1, parts, stations, tile), lambda c, i: (c, 0, 0, i)),
        ]
        + [ANY] * len(after),
        out_specs=pl.BlockSpec((1, 1, tile), lambda c, i: (c, 0, i)),
        compiler_params=params(),
        cost_estimate=cost(volt.size * beams * 4, volt.size * 2 + steer.size * 2),
        name="raw_power",
    )(volt, steer, *after)


def null_kernel(n_volt, own_ref, other_ref, raw_ref, steer_ref, *refs):
    volt_refs, out_ref, base_ref = refs[:n_volt], refs[n_volt], refs[n_volt + 1]
    channels, at = own_ref.shape[0], pl.program_id(0)

    @pl.when(at == 0)
    def _():
        made = orthonormal([images_of((own_ref, other_ref), c) for c in range(channels)])
        for c, (base_re, base_im) in enumerate(made):
            base_ref[c] = jnp.concatenate([base_re, base_im], 0)

    base = base_ref[at]
    base_re, base_im = split(base)
    number = base_re.shape[0]
    by_re = by_im = pairs = 0.0
    for ref in volt_refs:
        volt_re, volt_im = ref[at, 0], ref[at, 1]
        full = project(base_re, base_im, volt_re, volt_im).astype(BF16)
        by_re = by_re + contract(full, volt_re, 1, 0)
        by_im = by_im + contract(full, volt_im, 1, 0)
        pairs = pairs + contract(full, full, 1, 1)
    met = jnp.concatenate([by_re[:number] + by_im[number:], by_re[number:] - by_im[:number]], 0)
    high = met.astype(BF16)
    low = (met - high.astype(F32)).astype(BF16)
    left = jnp.concatenate([base.astype(BF16), high, low], 0)
    on_re = contract(left, steer_ref[0, 0], 1, 0)
    on_im = contract(left, steer_ref[0, 1], 1, 0)
    base_on_re, base_on_im = on_re[: 2 * number], on_im[: 2 * number]
    met_on_re = on_re[2 * number : 4 * number] + on_re[4 * number :]
    met_on_im = on_im[2 * number : 4 * number] + on_im[4 * number :]
    gain_re = base_on_re[:number] + base_on_im[number:]
    gain_im = base_on_re[number:] - base_on_im[:number]
    met_re = met_on_re[:number] - met_on_im[number:]
    met_im = met_on_im[:number] + met_on_re[number:]
    pair_re = pairs[:number, :number] + pairs[number:, number:]
    pair_im = pairs[:number, number:] - pairs[number:, :number]
    taken_re, taken_im = -2.0 * met_re, 2.0 * met_im
    for k in range(number):
        top_re, top_im = gain_re[k : k + 1], gain_im[k : k + 1]
        at_re, at_im = pair_re[:, k : k + 1], pair_im[:, k : k + 1]
        taken_re = taken_re + (at_re * top_re - at_im * top_im)
        taken_im = taken_im + (at_re * top_im + at_im * top_re)
    change = jnp.sum(gain_re * taken_re + gain_im * taken_im, axis=0, keepdims=True)
    for q in range(raw_ref.shape[0]):
        change = change + raw_ref[q, 0]
    out_ref[0] = change


def nulled_power(images, raw, volts, steer):
    own, other = images
    channels, parts, stations, beams = steer.shape
    moved = sum(v.size for v in volts)
    same = lambda v: pl.BlockSpec(v.shape, lambda i: (0,) * len(v.shape))
    return pl.pallas_call(
        functools.partial(null_kernel, len(volts)),
        out_shape=jax.ShapeDtypeStruct((channels, 1, beams), F32),
        grid=(channels,),
        in_specs=[
            same(own),
            same(other),
            pl.BlockSpec((raw.shape[0], 1, 1, beams), lambda i: (0, i, 0, 0)),
            pl.BlockSpec((1, parts, stations, beams), lambda i: (i, 0, 0, 0)),
        ]
        + [VMEM] * len(volts),
        out_specs=pl.BlockSpec((1, 1, beams), lambda i: (i, 0, 0)),
        scratch_shapes=[pltpu.VMEM(own.shape, F32)],
        compiler_params=params(),
        cost_estimate=cost(moved * 64 + steer.size * 96, moved * 2 + steer.size * 2),
        name="nulled_power",
    )(own, other, raw, steer, *volts)


def turn_series():
    nodes = np.cos((np.arange(4000) + 0.5) / 4000 * np.pi) * 0.25 + 0.25
    angle = 2.0 * np.pi * nodes
    fit = np.polynomial.chebyshev.Chebyshev.fit
    made = []
    for values, degree in ((np.cos(angle), 7), (np.sin(angle) / nodes, 6)):
        series = fit(nodes * nodes, values, degree, domain=[0, 0.25])
        made.append(series.convert(kind=np.polynomial.Polynomial).coef)
    return made


COS_SERIES, SIN_SERIES = turn_series()


def horner(at, series):
    total = jnp.float32(series[-1]) * at + jnp.float32(series[-2])
    for coef in series[-3::-1]:
        total = total * at + jnp.float32(coef)
    return total


def steer_kernel(freq_ref, place_ref, toward_ref, out_ref):
    delay = place_ref[:, 0:1] * toward_ref[0:1, :] + place_ref[:, 1:2] * toward_ref[1:2, :]
    for c in range(out_ref.shape[0]):
        turns = delay * freq_ref[c]
        rest = turns - jnp.round(turns)
        square = rest * rest
        out_ref[c, 0] = horner(square, COS_SERIES).astype(BF16)
        out_ref[c, 1] = (rest * horner(square, SIN_SERIES)).astype(BF16)


def steering(freq, places, toward, tile):
    channels, stations, beams = freq.shape[0], places.shape[0], toward.shape[1]
    return pl.pallas_call(
        steer_kernel,
        out_shape=jax.ShapeDtypeStruct((channels, 2, stations, beams), BF16),
        grid=(beams // tile,),
        in_specs=[
            SMEM,
            pl.BlockSpec((stations, 2), lambda i: (0, 0)),
            pl.BlockSpec((2, tile), lambda i: (0, i)),
        ],
        out_specs=pl.BlockSpec((channels, 2, stations, tile), lambda i: (0, 0, 0, i)),
        compiler_params=pltpu.CompilerParams(vmem_limit_bytes=VMEM_LIMIT),
        cost_estimate=pl.CostEstimate(
            flops=channels * stations * beams * 40,
            bytes_accessed=channels * stations * beams * 4,
            transcendentals=0,
        ),
        name="steering",
    )(freq, places, toward)


SWAP = [(0, 1), (1, 0)]


def patterns(group):
    bits = group.bit_length() - 1
    core = 2 if bits > 2 else 0
    wide = [p for p in range(group) if not p & core]
    every = group - 1 - core
    order = []
    for low in (0, core) if core else (0,):
        for p in sorted(wide, key=lambda w: (bin(w).count("1"), -w)):
            if 0 < p <= (p ^ every) or (p and not p ^ every):
                order.append(p | low)
                if p ^ every:
                    order.append((p ^ every) | low)
    order = list(dict.fromkeys(order))
    return order + [p for p in range(group - 1, -1, -1) if p not in order]


def body(volt, windows, start_basis, positions, pointing, beam_dir):
    parts, channels_all, rows, stations = volt.shape
    number = start_basis.shape[2]
    n_lo, n_time = lax.axis_size("lo"), lax.axis_size("tm")
    half_at, lo_at, time_at = (lax.axis_index(a) for a in ("hi", "lo", "tm"))
    group = n_lo * n_time
    chan_dev = windows.shape[0]
    per = chan_dev // n_time
    half_time = rows * group
    beams = beam_dir.shape[0]

    own_windows = lax.dynamic_slice_in_dim(windows, time_at * per, per, 0)
    own_basis = lax.dynamic_slice_in_dim(start_basis, time_at * per, per, 1)
    own_basis = jnp.transpose(own_basis, (1, 0, 2, 3)).reshape(per, parts * number, stations)
    far_windows = lax.ppermute(own_windows, "hi", SWAP)
    far_basis = lax.ppermute(own_basis, "hi", SWAP)
    lower = half_at == 0

    def by_owner(own, far):
        return jnp.concatenate([jnp.where(lower, own, far), jnp.where(lower, far, own)])

    blocks = volt.reshape(parts, 2, group, per, rows, stations)
    me = lo_at * n_time + time_at
    order = patterns(group)
    came = []
    for pattern in order:
        block = lax.dynamic_index_in_dim(blocks, me ^ pattern, 2, keepdims=False)
        if pattern:
            pairs = [(g, g ^ pattern) for g in range(group)]
            block = lax.ppermute(block, ("lo", "tm"), pairs)
        came.append(block)
    starts = half_at * half_time + (me ^ jnp.array(order, jnp.int32)) * rows
    times = starts[:, None] + jnp.arange(rows, dtype=jnp.int32)[None, :]
    times = times.astype(jnp.int32).reshape(1, half_time)

    toward = jnp.take(pointing, beam_dir, axis=1)
    ids = jnp.arange(per, dtype=jnp.int32) + (lo_at * chan_dev + time_at * per)
    channel_ids = jnp.concatenate([ids, ids + n_lo * chan_dev])
    freq = 1.0 + channel_ids.astype(F32) / channels_all
    steer = steering(freq, positions.T, toward, 128)

    share = group // QUARTERS
    volts, raw = [], []
    for q in range(QUARTERS):
        volts.append(pack(came[q * share : (q + 1) * share], tuple(raw[-1:])))
        if q < QUARTERS - 1:
            raw.append(raw_power(volts[q], steer, ()))

    far_windows, far_basis, _ = lax.optimization_barrier((far_windows, far_basis, raw[-1]))
    all_windows = by_owner(own_windows, far_windows)
    images = (by_owner(own_basis, far_basis),)
    after = ()
    for step in range(ITERS):
        image = iterate(all_windows, times, images, volts, after)
        images = (image, lax.ppermute(image, "hi", SWAP))
        after = ()
        if step == 0:
            raw.append(raw_power(volts[-1], steer, (image,)))
            after = (raw[-1],)
    power = nulled_power(images, jnp.stack(raw), volts, steer)
    mine = power.reshape(2, per, n_time, beams // n_time)
    mine = jnp.transpose(mine, (0, 2, 1, 3)) / (2 * half_time * stations)
    flat = mine.reshape(2 * n_time, per, beams // n_time)
    came = lax.all_to_all(flat, ("hi", "tm"), split_axis=0, concat_axis=0, tiled=True)
    came = came.reshape(2, n_time * per, beams // n_time)
    return came[0] + came[1]


def solution(mesh):
    n_chan, n_time = mesh.shape["chan"], mesh.shape["tm"]
    halves = Mesh(mesh.devices.reshape(2, n_chan // 2, n_time), ("hi", "lo", "tm"))
    chan = ("hi", "lo")
    return jax.shard_map(
        body,
        mesh=halves,
        in_specs=(
            P(None, None, ("hi", "lo", "tm"), None),
            P(chan, None),
            P(None, chan, None, None),
            P(),
            P(),
            P(),
        ),
        out_specs=P(chan, "tm"),
        check_vma=False,
    )
```

```python
import functools

import jax
import jax.numpy as jnp
import numpy as np
from jax import lax
from jax.experimental import pallas as pl
from jax.experimental.pallas import tpu as pltpu
from jax.sharding import Mesh
from jax.sharding import PartitionSpec as P

ITERS = 6
EPS = 1e-06
QUARTERS = 4
EARLY = 2
F32 = jnp.float32
BF16 = jnp.bfloat16
VMEM = pl.BlockSpec(memory_space=pltpu.VMEM)
SMEM = pl.BlockSpec(memory_space=pltpu.SMEM)
ANY = pl.BlockSpec(memory_space=pl.ANY)
VMEM_LIMIT = 24 << 20


def orthonormal(chans):
    number = chans[0][0].shape[0]
    row = lax.broadcasted_iota(jnp.int32, (number, 1), 0)
    for j in range(number):
        after = []
        for re, im in chans:
            top_re, top_im = re[j : j + 1], im[j : j + 1]
            dot_re = jnp.sum(top_re * re + top_im * im, axis=1, keepdims=True)
            dot_im = jnp.sum(top_re * im - top_im * re, axis=1, keepdims=True)
            inverse = lax.rsqrt(dot_re[j : j + 1] + EPS)
            share = jnp.where(row > j, inverse * inverse, 0.0)
            coef_re, coef_im = share * dot_re, share * dot_im
            scale = jnp.where(row == j, inverse, 1.0)
            after.append(
                (
                    re * scale - (coef_re * top_re - coef_im * top_im),
                    im * scale - (coef_re * top_im + coef_im * top_re),
                )
            )
        chans = after
    return chans


def contract(left, right, at_left, at_right):
    return lax.dot_general(
        left, right, (((at_left,), (at_right,)), ((), ())), preferred_element_type=F32
    )


def project(base_re, base_im, volt_re, volt_im):
    first = jnp.concatenate([base_re, -base_im], 0).astype(BF16)
    second = jnp.concatenate([base_im, base_re], 0).astype(BF16)
    return contract(first, volt_re, 1, 1) + contract(second, volt_im, 1, 1)


def split(stacked):
    number = stacked.shape[0] // 2
    return stacked[:number], stacked[number:]


def images_of(image_refs, at):
    total = image_refs[0][at].astype(F32)
    for ref in image_refs[1:]:
        total = total + ref[at].astype(F32)
    return split(total)


def params(limit=VMEM_LIMIT):
    return pltpu.CompilerParams(vmem_limit_bytes=limit)


def cost(flops, moved):
    return pl.CostEstimate(flops=int(flops), bytes_accessed=int(moved), transcendentals=0)


def pack_kernel(n_blocks, *refs):
    block_refs, out_ref = refs[:n_blocks], refs[-1]
    parts, owners, per, rows, _ = block_refs[0].shape
    for j, ref in enumerate(block_refs):
        for owner in range(owners):
            for i in range(per):
                for part in range(parts):
                    out_ref[owner * per + i, part, j * rows : (j + 1) * rows] = ref[part, owner, i]


def pack(blocks, after):
    parts, owners, per, rows, stations = blocks[0].shape
    shape = (owners * per, parts, len(blocks) * rows, stations)
    return pl.pallas_call(
        functools.partial(pack_kernel, len(blocks)),
        out_shape=jax.ShapeDtypeStruct(shape, BF16),
        in_specs=[VMEM] * len(blocks) + [ANY] * len(after),
        out_specs=VMEM,
        compiler_params=params(),
        cost_estimate=cost(0, 4 * len(blocks) * blocks[0].size),
        name="pack",
    )(*blocks, *after)


def joined(volt_refs, channel, part):
    return jnp.concatenate([ref[channel, part] for ref in volt_refs], 0)


def iterate_kernel(n_images, n_volt, win_ref, *refs):
    image_refs, times_ref = refs[:n_images], refs[n_images]
    volt_refs, out_ref = refs[n_images + 1 : n_images + 1 + n_volt], refs[-1]
    channels, number = out_ref.shape[0], out_ref.shape[1] // 2
    bases = orthonormal([images_of(image_refs, c) for c in range(channels)])
    for c in range(channels):
        volt_re, volt_im = (joined(volt_refs, c, part) for part in range(2))
        proj = project(*bases[c], volt_re, volt_im)
        sample = times_ref[...]
        inside = (sample >= win_ref[c, 0]) & (sample < win_ref[c, 1])
        proj = jnp.where(inside, proj, 0.0).astype(BF16)
        by_re, by_im = contract(proj, volt_re, 1, 0), contract(proj, volt_im, 1, 0)
        out_ref[c, :number] = (by_re[:number] - by_im[number:]).astype(out_ref.dtype)
        out_ref[c, number:] = (by_im[:number] + by_re[number:]).astype(out_ref.dtype)


def iterate(windows, times, images, volts, after):
    moved = sum(v.size for v in volts)
    return pl.pallas_call(
        functools.partial(iterate_kernel, len(images), len(volts)),
        out_shape=jax.ShapeDtypeStruct(images[0].shape, BF16),
        in_specs=[SMEM] + [VMEM] * (len(images) + 1 + len(volts)) + [ANY] * len(after),
        out_specs=VMEM,
        compiler_params=params(),
        cost_estimate=cost(moved * 64, moved * 2),
        name="iterate",
    )(windows, *images, times, *volts, *after)


def raw_kernel(volt_ref, steer_ref, *refs):
    out_ref = refs[-1]
    _, parts, rows, stations = volt_ref.shape
    volt = volt_ref[0].reshape(parts * rows, stations)
    on_re, on_im = contract(volt, steer_ref[0, 0], 1, 0), contract(volt, steer_ref[0, 1], 1, 0)
    beam_re = on_re[:rows] + on_im[rows:]
    beam_im = on_re[rows:] - on_im[:rows]
    out_ref[0] = jnp.sum(beam_re * beam_re + beam_im * beam_im, axis=0, keepdims=True)


def raw_power(volt, steer, after, first=0, channels=None):
    _, parts, rows, stations = volt.shape
    channels = channels or volt.shape[0]
    beams = steer.shape[-1]
    tile = min(512, beams)
    return pl.pallas_call(
        raw_kernel,
        out_shape=jax.ShapeDtypeStruct((channels, 1, beams), F32),
        grid=(channels, beams // tile),
        in_specs=[
            pl.BlockSpec((1, parts, rows, stations), lambda c, i: (first + c, 0, 0, 0)),
            pl.BlockSpec((1, parts, stations, tile), lambda c, i: (first + c, 0, 0, i)),
        ]
        + [ANY] * len(after),
        out_specs=pl.BlockSpec((1, 1, tile), lambda c, i: (c, 0, i)),
        compiler_params=params(),
        cost_estimate=cost(
            channels * parts * rows * stations * beams * 4,
            channels * parts * stations * (rows + beams) * 2,
        ),
        name="raw_power",
    )(volt, steer, *after)


def null_kernel(n_volt, own_ref, other_ref, raw_ref, steer_ref, *refs):
    volt_refs, out_ref, base_ref = refs[:n_volt], refs[n_volt], refs[n_volt + 1]
    channels, at = own_ref.shape[0], pl.program_id(0)

    @pl.when(at == 0)
    def _():
        made = orthonormal([images_of((own_ref, other_ref), c) for c in range(channels)])
        for c, (base_re, base_im) in enumerate(made):
            base_ref[c] = jnp.concatenate([base_re, base_im], 0)

    base = base_ref[at]
    base_re, base_im = split(base)
    number = base_re.shape[0]
    volt_re, volt_im = (joined(volt_refs, at, part) for part in range(2))
    full = project(base_re, base_im, volt_re, volt_im).astype(BF16)
    by_re, by_im = contract(full, volt_re, 1, 0), contract(full, volt_im, 1, 0)
    pairs = contract(full, full, 1, 1)
    met = jnp.concatenate([by_re[:number] + by_im[number:], by_re[number:] - by_im[:number]], 0)
    high = met.astype(BF16)
    low = (met - high.astype(F32)).astype(BF16)
    left = jnp.concatenate([base.astype(BF16), high, low], 0)
    on_re = contract(left, steer_ref[0, 0], 1, 0)
    on_im = contract(left, steer_ref[0, 1], 1, 0)
    base_on_re, base_on_im = on_re[: 2 * number], on_im[: 2 * number]
    met_on_re = on_re[2 * number : 4 * number] + on_re[4 * number :]
    met_on_im = on_im[2 * number : 4 * number] + on_im[4 * number :]
    gain_re = base_on_re[:number] + base_on_im[number:]
    gain_im = base_on_re[number:] - base_on_im[:number]
    met_re = met_on_re[:number] - met_on_im[number:]
    met_im = met_on_im[:number] + met_on_re[number:]
    pair_re = pairs[:number, :number] + pairs[number:, number:]
    pair_im = pairs[:number, number:] - pairs[number:, :number]
    taken_re, taken_im = -2.0 * met_re, 2.0 * met_im
    for k in range(number):
        top_re, top_im = gain_re[k : k + 1], gain_im[k : k + 1]
        at_re, at_im = pair_re[:, k : k + 1], pair_im[:, k : k + 1]
        taken_re = taken_re + (at_re * top_re - at_im * top_im)
        taken_im = taken_im + (at_re * top_im + at_im * top_re)
    change = jnp.sum(gain_re * taken_re + gain_im * taken_im, axis=0, keepdims=True)
    for q in range(raw_ref.shape[0]):
        change = change + raw_ref[q, 0]
    out_ref[0] = change


def nulled_power(images, raw, volts, steer):
    own, other = images
    channels, parts, stations, beams = steer.shape
    moved = sum(v.size for v in volts)
    same = lambda v: pl.BlockSpec(v.shape, lambda i: (0,) * len(v.shape))
    return pl.pallas_call(
        functools.partial(null_kernel, len(volts)),
        out_shape=jax.ShapeDtypeStruct((channels, 1, beams), F32),
        grid=(channels,),
        in_specs=[
            same(own),
            same(other),
            pl.BlockSpec((raw.shape[0], 1, 1, beams), lambda i: (0, i, 0, 0)),
            pl.BlockSpec((1, parts, stations, beams), lambda i: (i, 0, 0, 0)),
        ]
        + [VMEM] * len(volts),
        out_specs=pl.BlockSpec((1, 1, beams), lambda i: (i, 0, 0)),
        scratch_shapes=[pltpu.VMEM(own.shape, F32)],
        compiler_params=params(),
        cost_estimate=cost(moved * 64 + steer.size * 96, moved * 2 + steer.size * 2),
        name="nulled_power",
    )(own, other, raw, steer, *volts)


def turn_series():
    nodes = np.cos((np.arange(4000) + 0.5) / 4000 * np.pi) * 0.25 + 0.25
    angle = 2.0 * np.pi * nodes
    fit = np.polynomial.chebyshev.Chebyshev.fit
    made = []
    for values, degree in ((np.cos(angle), 7), (np.sin(angle) / nodes, 6)):
        series = fit(nodes * nodes, values, degree, domain=[0, 0.25])
        made.append(series.convert(kind=np.polynomial.Polynomial).coef)
    return made


COS_SERIES, SIN_SERIES = turn_series()


def horner(at, series):
    total = jnp.float32(series[-1]) * at + jnp.float32(series[-2])
    for coef in series[-3::-1]:
        total = total * at + jnp.float32(coef)
    return total


def steer_kernel(freq_ref, place_ref, toward_ref, out_ref):
    delay = place_ref[:, 0:1] * toward_ref[0:1, :] + place_ref[:, 1:2] * toward_ref[1:2, :]
    for c in range(out_ref.shape[0]):
        turns = delay * freq_ref[c]
        rest = turns - jnp.round(turns)
        square = rest * rest
        out_ref[c, 0] = horner(square, COS_SERIES).astype(BF16)
        out_ref[c, 1] = (rest * horner(square, SIN_SERIES)).astype(BF16)


def steering(freq, places, toward, tile):
    channels, stations, beams = freq.shape[0], places.shape[0], toward.shape[1]
    return pl.pallas_call(
        steer_kernel,
        out_shape=jax.ShapeDtypeStruct((channels, 2, stations, beams), BF16),
        grid=(beams // tile,),
        in_specs=[
            SMEM,
            pl.BlockSpec((stations, 2), lambda i: (0, 0)),
            pl.BlockSpec((2, tile), lambda i: (0, i)),
        ],
        out_specs=pl.BlockSpec((channels, 2, stations, tile), lambda i: (0, 0, 0, i)),
        compiler_params=pltpu.CompilerParams(vmem_limit_bytes=VMEM_LIMIT),
        cost_estimate=pl.CostEstimate(
            flops=channels * stations * beams * 40,
            bytes_accessed=channels * stations * beams * 4,
            transcendentals=0,
        ),
        name="steering",
    )(freq, places, toward)


SWAP = [(0, 1), (1, 0)]


def patterns(group):
    bits = group.bit_length() - 1
    core = 2 if bits > 2 else 0
    wide = [p for p in range(group) if not p & core]
    every = group - 1 - core
    order = []
    for low in (0, core) if core else (0,):
        for p in sorted(wide, key=lambda w: (bin(w).count("1"), -w)):
            if 0 < p <= (p ^ every) or (p and not p ^ every):
                order.append(p | low)
                if p ^ every:
                    order.append((p ^ every) | low)
    order = list(dict.fromkeys(order))
    return order + [p for p in range(group - 1, -1, -1) if p not in order]


def body(volt, windows, start_basis, positions, pointing, beam_dir):
    parts, channels_all, rows, stations = volt.shape
    number = start_basis.shape[2]
    n_lo, n_time = lax.axis_size("lo"), lax.axis_size("tm")
    half_at, lo_at, time_at = (lax.axis_index(a) for a in ("hi", "lo", "tm"))
    group = n_lo * n_time
    chan_dev = windows.shape[0]
    per = chan_dev // n_time
    half_time = rows * group
    beams = beam_dir.shape[0]

    own_windows = lax.dynamic_slice_in_dim(windows, time_at * per, per, 0)
    own_basis = lax.dynamic_slice_in_dim(start_basis, time_at * per, per, 1)
    own_basis = jnp.transpose(own_basis, (1, 0, 2, 3)).reshape(per, parts * number, stations)
    marks = jnp.pad(own_windows.astype(F32)[:, None], ((0, 0), (0, 0), (0, stations - 2)))
    own = jnp.concatenate([own_basis, marks], 1)
    far = lax.ppermute(own, "hi", SWAP)
    lower = half_at == 0
    both = jnp.concatenate([jnp.where(lower, own, far), jnp.where(lower, far, own)])
    images = (both[:, :-1],)
    all_windows = both[:, -1, :2].astype(jnp.int32)

    blocks = volt.reshape(parts, 2, group, per, rows, stations)
    me = lo_at * n_time + time_at
    order = patterns(group)
    came = []
    for k, pattern in enumerate(order):
        block = lax.dynamic_index_in_dim(blocks, me ^ pattern, 2, keepdims=False)
        came.append(block)
        if k == EARLY - 1:
            *came, blocks = lax.optimization_barrier((*came, blocks))
    for k, pattern in enumerate(order):
        if pattern:
            pairs = [(g, g ^ pattern) for g in range(group)]
            came[k] = lax.ppermute(came[k], ("lo", "tm"), pairs)
    starts = half_at * half_time + (me ^ jnp.array(order, jnp.int32)) * rows
    times = starts[:, None] + jnp.arange(rows, dtype=jnp.int32)[None, :]
    times = times.astype(jnp.int32).reshape(1, half_time)

    toward = jnp.take(pointing, beam_dir, axis=1)
    ids = jnp.arange(per, dtype=jnp.int32) + (lo_at * chan_dev + time_at * per)
    channel_ids = jnp.concatenate([ids, ids + n_lo * chan_dev])
    freq = 1.0 + channel_ids.astype(F32) / channels_all
    steer = steering(freq, positions.T, toward, 128)

    share = group // QUARTERS
    volts, raw = [], []
    for q in range(QUARTERS):
        volts.append(pack(came[q * share : (q + 1) * share], tuple(raw[-1:])))
        if q < QUARTERS - 1:
            raw.append(raw_power(volts[q], steer, ()))

    after, late = (), []
    for step in range(ITERS):
        image = iterate(all_windows, times, images, volts, after)
        images = (image, lax.ppermute(image, "hi", SWAP))
        after = ()
        if step < 2:
            late.append(raw_power(volts[-1], steer, (image,), step * per, per))
            after = (late[-1],)
    raw.append(jnp.concatenate(late))
    power = nulled_power(images, jnp.stack(raw), volts, steer)
    mine = power.reshape(2, per, n_time, beams // n_time)
    mine = jnp.transpose(mine, (0, 2, 1, 3)) / (2 * half_time * stations)
    flat = mine.reshape(2 * n_time, per, beams // n_time)
    came = lax.all_to_all(flat, ("hi", "tm"), split_axis=0, concat_axis=0, tiled=True)
    came = came.reshape(2, n_time * per, beams // n_time)
    return came[0] + came[1]


def solution(mesh):
    n_chan, n_time = mesh.shape["chan"], mesh.shape["tm"]
    halves = Mesh(mesh.devices.reshape(2, n_chan // 2, n_time), ("hi", "lo", "tm"))
    chan = ("hi", "lo")
    return jax.shard_map(
        body,
        mesh=halves,
        in_specs=(
            P(None, None, ("hi", "lo", "tm"), None),
            P(chan, None),
            P(None, chan, None, None),
            P(),
            P(),
            P(),
        ),
        out_specs=P(chan, "tm"),
        check_vma=False,
    )
```
